32 devices in a mesh: grp: 4 (over y, core), inner: 8 (over z, x).
Axes of the slice: x: 2, y: 2, z: 4, core: 2. Of those that a mesh axis runs over, the one named last changes fastest.
Arguments:
- grad_out: bfloat16 [4096, 2048], P(('grp', 'inner')), may hold values from -6 to 6
- hidden: bfloat16 [4096, 2048], P(('grp', 'inner')), may hold values from -6 to 6
- norm_gain: float32 [2048], replicated, may hold values from 0.25 to 1.75
- expert_ids: int32 [4096, 8], P(('grp', 'inner')), may hold values from 0 to 31, all different within a row; in each aligned block of 128 rows (0 to 127, 128 to 255, ...) at most 40 rows name the same one
- gate_weights: float32 [4096, 8], P(('grp', 'inner')), may hold values from 0.02 to 0.5
- w_gate: bfloat16 [32, 2048, 768], P(('grp', 'inner')), may hold values from -0.125 to 0.125
- w_up: bfloat16 [32, 2048, 768], P(('grp', 'inner')), may hold values from -0.125 to 0.125
- w_down: bfloat16 [32, 768, 2048], P(('grp', 'inner')), may hold values from -0.21875 to 0.21875
- w_out: bfloat16 [4096, 2048], P('inner'), may hold values from -0.09375 to 0.09375
- queries: bfloat16 [4096, 4096], P(('grp', 'inner')), may hold values from -0.6 to 0.6
- keys: bfloat16 [4096, 512], P(('grp', 'inner')), may hold values from -0.6 to 0.6
- values: bfloat16 [4096, 512], P(('grp', 'inner')), may hold values from -6 to 6
- attn_out: bfloat16 [4096, 4096], P(('grp', 'inner')), may hold values from -6 to 6
- lse: float32 [32, 4096], P('inner', 'grp'), as said below
Outputs:
- grad_resid: bfloat16 [4096, 2048], P(('grp', 'inner'))
- queries_gradient: bfloat16 [4096, 4096], P(('grp', 'inner'))
- keys_gradient: bfloat16 [4096, 512], P(('grp', 'inner'))
- values_gradient: bfloat16 [4096, 512], P(('grp', 'inner'))
The draws below stay inside these ranges and needn't reach their ends.
Inputs may be any that keep to these rules, and one draw needn't show every extreme that they name: `expert_ids`: each token names 8 different experts. Among the 128 tokens of one device (aligned blocks of rows), no expert is named by more than 40 tokens; in some device's tokens one expert is named by exactly 40. lse[h, t] minus log(1 + the position of token t in its sequence of 1024) lies between 0 and 1.5.
All inputs are finite; a program needn't handle non-finite values.
Results may differ from the reference program's by a relative error of at most 0.012.
Values may be sent and summed in bfloat16 or wider, within the bound.
A program may use at most 192 MiB of HBM per device.

```python
import math
import jax
import jax.numpy as jnp
import numpy as np
from jax import lax

D = 2048
QUERY_HEADS = 32
KEY_VALUE_HEADS = 4
HEAD_SIZE = 128
FF = 768
TOPK = 8
TOK_DEV = 128
EXPERTS = 32
CAP = 40
SEQUENCE_TOKENS = 1024
TOTAL_TOKENS = 4096


def draw_lse(key, part):
    position = (jnp.arange(TOTAL_TOKENS, dtype=jnp.int32) % SEQUENCE_TOKENS).astype(jnp.float32)
    base = jnp.log(position + 1.0)[None, :]
    extra = jax.random.uniform(key, (QUERY_HEADS, TOTAL_TOKENS), jnp.float32, 0.3, 1.2)
    return base + extra


def bounded_rows(key, columns):
    second = jax.random.fold_in(key, 23)
    drawn = jax.random.uniform(second, (TOTAL_TOKENS, columns), jnp.float32, -0.59, 0.59)
    return drawn.astype(jnp.bfloat16)


def draw_queries(key, part):
    return bounded_rows(jax.random.fold_in(key, 101), QUERY_HEADS * HEAD_SIZE)


def draw_keys(key, part):
    return bounded_rows(jax.random.fold_in(key, 202), KEY_VALUE_HEADS * HEAD_SIZE)


def shard_levels(own_key, shape, pieces, least, top_value):
    def one(dim, blocks):
        draws = jax.random.uniform(jax.random.fold_in(jax.random.fold_in(own_key, 6), dim), (blocks,), jnp.float32, least / len(pieces), top_value / len(pieces))
        return jnp.repeat(jnp.exp(draws), shape[dim] // blocks).reshape((-1,) + (1,) * (len(shape) - dim - 1))

    factor_of = one(*pieces[0])
    for cut in pieces[1:]:
        factor_of = factor_of * one(*cut)
    return factor_of


def shared_out(rng, own, number, rows, count, top, most, skew):
    order = jax.random.permutation(rng, count)
    crowded, usual = load_shares(count, rows * top, most, skew, True), load_shares(count, rows * top, most, skew, False)
    places = jnp.arange(count)

    def named(tallies, turn):
        used = int((tallies > 0).sum())
        fixed = max(1, used // 4)
        moved = fixed + (places - fixed + turn * (used - fixed)) % max(1, count - fixed)
        return jnp.zeros((count,), jnp.int32).at[order[jnp.where(places < fixed, places, moved)]].set(jnp.asarray(tallies, jnp.int32))

    tallies = jnp.where(number % 4 == 0, named(crowded, number // 4), named(usual, number - number // 4 - 1))
    mixed = jax.random.permutation(jax.random.fold_in(own, 3), count)
    giver, receiver = mixed[0:count // 2 * 2:2], mixed[1:count // 2 * 2:2]
    slack = jnp.minimum(tallies[giver] - 1, most - tallies[receiver]) // 2
    slack = jnp.where((giver == order[0]) | (receiver == order[0]) | (tallies[receiver] == 0), 0, jnp.maximum(slack, 0))
    moved = jax.random.randint(jax.random.fold_in(own, 4), (count // 2,), 0, 1 << 20) % (slack + 1)
    tallies = tallies.at[giver].add(-moved).at[receiver].add(moved)
    members = jnp.searchsorted(jnp.cumsum(tallies), jnp.arange(rows * top), side="right").astype(jnp.int32)
    grid = members.reshape(top, rows).T
    grid = grid[jax.random.permutation(jax.random.fold_in(own, 1), rows)]
    turn = jax.random.randint(jax.random.fold_in(own, 2), (rows, 1), 0, top)
    return jnp.take_along_axis(grid, (jnp.arange(top)[None, :] + turn) % top, axis=1)


def load_shares(count, total, reach, slope, full):
    loads = [(1 << 20) // math.isqrt(grade ** slope) + 1 for grade in range(1, count + 1)]
    largest = reach if full else min(reach, max(-(-total // count), total * loads[0] // sum(loads)))
    least = 1 if total - largest >= count - 1 else 0
    given, surplus = [largest] + [least] * (count - 1), total - largest - least * (count - 1)
    while surplus > 0:
        movable = [i for i in range(1, count) if given[i] < largest] or [i for i in range(1, count) if given[i] < reach]
        pool, left = sum([loads[i] for i in movable]), surplus
        for i in movable:
            more = min(reach - given[i], max(1, left * loads[i] // pool), surplus)
            given[i] = given[i] + more
            surplus = surplus - more
    return np.array(given)


def normal_values(key, extent, width, bound, pieces=(), kind=jnp.bfloat16):
    values = jax.random.normal(key, extent, jnp.float32) * width
    if len(pieces) > 0:
        values = shard_levels(key, extent, pieces, -0.22, 0.18) * values
    return jnp.clip(values, min=-bound, max=bound).astype(kind)


def setup_inputs(seed: int = 0) -> dict:
    splits = jax.random.split(jax.random.key(seed), 15)
    grad_out = normal_values(splits[0], (TOTAL_TOKENS, D), 1.0, 6.0, ((0, 32),))
    hidden = normal_values(splits[1], (TOTAL_TOKENS, D), 1.0, 6.0, ((0, 32),))
    norm_gain = jnp.clip(1.0 + 0.15 * jax.random.normal(splits[2], (D,), jnp.float32), 0.25, 1.75)
    expert_ids_keys = jax.random.split(jax.random.fold_in(splits[3], 1), TOTAL_TOKENS // TOK_DEV)
    expert_ids_turns = jax.random.permutation(jax.random.fold_in(splits[3], 3), TOTAL_TOKENS // TOK_DEV)
    expert_ids = jax.vmap(lambda own, number: shared_out(jax.random.fold_in(splits[3], 2), own, number, TOK_DEV, EXPERTS, TOPK, CAP, 1))(expert_ids_keys, expert_ids_turns).reshape((TOTAL_TOKENS, TOPK))
    gate_weights = jnp.clip(jnp.exp(math.log(0.5) - 3.218876 * jax.random.uniform(splits[4], (TOTAL_TOKENS, TOPK), jnp.float32) ** shard_levels(splits[4], (TOTAL_TOKENS, TOPK), ((0, 32),), -0.2, 0.2)), 0.02, 0.5)
    w_gate = normal_values(splits[5], (EXPERTS, D, FF), D ** -0.5, 0.125, ((0, 32),))
    w_up = normal_values(splits[6], (EXPERTS, D, FF), D ** -0.5, 0.125, ((0, 32),))
    w_down = normal_values(splits[7], (EXPERTS, FF, D), FF ** -0.5, 0.21875, ((0, 32),))
    w_out = normal_values(splits[8], (QUERY_HEADS * HEAD_SIZE, D), (QUERY_HEADS * HEAD_SIZE) ** -0.5, 0.09375, ((0, 8),))
    queries = draw_queries(jax.random.fold_in(splits[14], 71), 0)
    keys = draw_keys(jax.random.fold_in(splits[14], 71), 0)
    values = normal_values(splits[11], (TOTAL_TOKENS, KEY_VALUE_HEADS * HEAD_SIZE), 1.0, 6.0, ((0, 32),))
    attn_out = normal_values(splits[12], (TOTAL_TOKENS, QUERY_HEADS * HEAD_SIZE), 1.0, 6.0, ((0, 32),))
    lse = draw_lse(jax.random.fold_in(splits[14], 71), 0)
    return {"grad_out": grad_out, "hidden": hidden, "norm_gain": norm_gain, "expert_ids": expert_ids, "gate_weights": gate_weights, "w_gate": w_gate, "w_up": w_up, "w_down": w_down, "w_out": w_out, "queries": queries, "keys": keys, "values": values, "attn_out": attn_out, "lse": lse}


def contract_last(left, right):
    return lax.dot_general(left, right, (((1,), (1,)), ((), ())), preferred_element_type=jnp.float32)

def expert_back(inputs, upstream, gate_matrix, up_matrix, down_matrix):
    gate_pre = jnp.dot(inputs, gate_matrix, preferred_element_type=jnp.float32)
    up_pre = jnp.dot(inputs, up_matrix, preferred_element_type=jnp.float32)
    back_hidden = contract_last(upstream, down_matrix)
    sigmoid = jax.nn.sigmoid(gate_pre)
    grad_gate = (back_hidden * up_pre * sigmoid * (1.0 + gate_pre * (1.0 - sigmoid))).astype(jnp.bfloat16)
    grad_up = (back_hidden * gate_pre * sigmoid).astype(jnp.bfloat16)
    grad_in = contract_last(grad_gate, gate_matrix) + contract_last(grad_up, up_matrix)
    return grad_in.astype(jnp.bfloat16)

def head_group(operands):
    query_blk, output_blk, grad_blk, key_blk, value_blk, lse_blk = operands
    scale = float(HEAD_SIZE) ** (-0.5)
    query_f = query_blk.astype(jnp.float32)
    key_f = key_blk.astype(jnp.float32)
    value_f = value_blk.astype(jnp.float32)
    grad_f = grad_blk.astype(jnp.float32)
    output_f = output_blk.astype(jnp.float32)
    scores = jnp.einsum('gid,jd->gij', query_f, key_f) * scale
    position = jnp.arange(SEQUENCE_TOKENS, dtype=jnp.int32)
    visible = position[None, :] <= position[:, None]
    probs = jnp.where(visible[None], jnp.exp(scores - lse_blk[:, :, None]), 0.0)
    probs_low = probs.astype(jnp.bfloat16).astype(jnp.float32)
    grad_probs = jnp.einsum('gid,jd->gij', grad_f, value_f)
    delta = lax.optimization_barrier(jnp.sum(grad_f * output_f, axis=-1))
    grad_scores = (probs * (grad_probs - delta[:, :, None])).astype(jnp.bfloat16).astype(jnp.float32)
    query_gradient_fn = jnp.einsum('gij,jd->gid', grad_scores, key_f) * scale
    key_gradient_fn = jnp.einsum('gij,gid->jd', grad_scores, query_f) * scale
    value_gradient_fn = jnp.einsum('gij,gid->jd', probs_low, grad_f)
    return (query_gradient_fn.astype(jnp.bfloat16), key_gradient_fn.astype(jnp.bfloat16), value_gradient_fn.astype(jnp.bfloat16))

def reference(grad_out, hidden, norm_gain, expert_ids, gate_weights, w_gate, w_up, w_down, w_out, queries, keys, values, attn_out, lse):
    hidden_f = hidden.astype(jnp.float32)
    inverse = lax.rsqrt(lax.optimization_barrier(jnp.mean(hidden_f * hidden_f, axis=1, keepdims=True)) + 1e-06)
    normed = (hidden_f * inverse * norm_gain).astype(jnp.bfloat16)
    upstream = grad_out.astype(jnp.float32)
    flat_count = TOTAL_TOKENS * TOPK
    flat_ids = expert_ids.reshape(-1)
    flat_weights = gate_weights.reshape(-1)
    order = jnp.argsort(flat_ids, stable=True).astype(jnp.int32)
    counts = lax.optimization_barrier(jnp.sum((flat_ids[:, None] == jnp.arange(EXPERTS, dtype=jnp.int32)[None, :]).astype(jnp.int32), axis=0))
    starts = jnp.cumsum(counts) - counts
    most = TOTAL_TOKENS // TOK_DEV * CAP

    def one_expert(total, expert):
        offsets = jnp.arange(most, dtype=jnp.int32)
        place = starts[expert] + offsets
        valid = offsets < counts[expert]
        rows = order[jnp.minimum(place, flat_count - 1)]
        tok_index = rows // TOPK
        inputs = normed[tok_index]
        scaled = (upstream[tok_index] * flat_weights[rows][:, None]).astype(jnp.bfloat16)
        grad_in = expert_back(inputs, scaled, w_gate[expert], w_up[expert], w_down[expert])
        grad_in = jnp.where(valid[:, None], grad_in.astype(jnp.float32), 0.0)
        return (total.at[tok_index].add(grad_in), None)
    grad_normed, _ = lax.scan(one_expert, jnp.zeros((TOTAL_TOKENS, D), jnp.float32), jnp.arange(EXPERTS, dtype=jnp.int32))
    gained = grad_normed * norm_gain
    statistic = lax.optimization_barrier(jnp.mean(gained * hidden_f, axis=1, keepdims=True))
    grad_resid = (upstream + inverse * gained - hidden_f * inverse * inverse * inverse * statistic).astype(jnp.bfloat16)
    grad_attn = contract_last(grad_resid, w_out).astype(jnp.bfloat16)
    sequence_count = TOTAL_TOKENS // SEQUENCE_TOKENS
    shared_result = QUERY_HEADS // KEY_VALUE_HEADS

    def by_head(numeric_array):
        return numeric_array.reshape(sequence_count, SEQUENCE_TOKENS, KEY_VALUE_HEADS, shared_result, HEAD_SIZE).transpose(0, 2, 3, 1, 4).reshape(sequence_count * KEY_VALUE_HEADS, shared_result, SEQUENCE_TOKENS, HEAD_SIZE)

    def by_kv(numeric_array):
        return numeric_array.reshape(sequence_count, SEQUENCE_TOKENS, KEY_VALUE_HEADS, HEAD_SIZE).transpose(0, 2, 1, 3).reshape(sequence_count * KEY_VALUE_HEADS, SEQUENCE_TOKENS, HEAD_SIZE)
    logsumexp_heads = lse.reshape(KEY_VALUE_HEADS, shared_result, sequence_count, SEQUENCE_TOKENS).transpose(2, 0, 1, 3).reshape(sequence_count * KEY_VALUE_HEADS, shared_result, SEQUENCE_TOKENS)
    query_gradient_fn, key_gradient_fn, value_gradient_fn = lax.map(head_group, (by_head(queries), by_head(attn_out), by_head(grad_attn), by_kv(keys), by_kv(values), logsumexp_heads))
    queries_gradient = query_gradient_fn.reshape(sequence_count, KEY_VALUE_HEADS, shared_result, SEQUENCE_TOKENS, HEAD_SIZE).transpose(0, 3, 1, 2, 4).reshape(TOTAL_TOKENS, QUERY_HEADS * HEAD_SIZE)
    keys_gradient = key_gradient_fn.reshape(sequence_count, KEY_VALUE_HEADS, SEQUENCE_TOKENS, HEAD_SIZE).transpose(0, 2, 1, 3).reshape(TOTAL_TOKENS, KEY_VALUE_HEADS * HEAD_SIZE)
    values_gradient = value_gradient_fn.reshape(sequence_count, KEY_VALUE_HEADS, SEQUENCE_TOKENS, HEAD_SIZE).transpose(0, 2, 1, 3).reshape(TOTAL_TOKENS, KEY_VALUE_HEADS * HEAD_SIZE)
    return (grad_resid, queries_gradient, keys_gradient, values_gradient)
```

```python
import functools

import jax
import jax.numpy as jnp
from jax import lax
from jax.experimental import pallas as pl
from jax.experimental.pallas import tpu as pltpu
from jax.sharding import PartitionSpec as P

KEY_VALUE_HEADS = 4
HEAD_SIZE = 128


EPSILON = 1e-06


def contract_last(left, right):
    return lax.dot_general(
        left, right, (((1,), (1,)), ((), ())), preferred_element_type=jnp.float32
    )


def contract_first(left, right):
    return lax.dot_general(
        left, right, (((0,), (0,)), ((), ())), preferred_element_type=jnp.float32
    )


def expert_rows_grads(inputs, upstream, gate_matrix, up_matrix, down_matrix):
    gate_pre = jnp.dot(inputs, gate_matrix, preferred_element_type=jnp.float32)
    up_pre = jnp.dot(inputs, up_matrix, preferred_element_type=jnp.float32)
    back_hidden = contract_last(upstream, down_matrix)
    sigmoid = jax.nn.sigmoid(gate_pre)
    grad_gate = (back_hidden * up_pre * sigmoid * (1.0 + gate_pre * (1.0 - sigmoid))).astype(
        jnp.bfloat16
    )
    grad_up = (back_hidden * gate_pre * sigmoid).astype(jnp.bfloat16)
    grad_in = contract_last(grad_gate, gate_matrix) + contract_last(grad_up, up_matrix)
    return grad_in.astype(jnp.bfloat16)


def expert_grads(received, w_gate, w_up, w_down):
    local = w_gate.shape[0]
    width = w_gate.shape[1]
    shaped = received.reshape((-1, local) + received.shape[1:])
    inputs = shaped[..., :width]
    upstream = shaped[..., width:]
    gate_pre = jnp.einsum("nlcd,ldf->nlcf", inputs, w_gate, preferred_element_type=jnp.float32)
    up_pre = jnp.einsum("nlcd,ldf->nlcf", inputs, w_up, preferred_element_type=jnp.float32)
    back_hidden = jnp.einsum("nlcd,lfd->nlcf", upstream, w_down, preferred_element_type=jnp.float32)
    sigmoid = jax.nn.sigmoid(gate_pre)
    grad_gate = (back_hidden * up_pre * sigmoid * (1.0 + gate_pre * (1.0 - sigmoid))).astype(
        jnp.bfloat16
    )
    grad_up = (back_hidden * gate_pre * sigmoid).astype(jnp.bfloat16)
    grad_in = jnp.einsum("nlcf,ldf->nlcd", grad_gate, w_gate, preferred_element_type=jnp.float32)
    grad_in = grad_in + jnp.einsum(
        "nlcf,ldf->nlcd", grad_up, w_up, preferred_element_type=jnp.float32
    )
    return grad_in.astype(jnp.bfloat16).reshape(received.shape[:-1] + (width,))


MESH_ID = pl.DeviceIdType.MESH
GATHER_LIMIT = 48 * 2**20


def spread_kernel(
    cols,
    lines,
    first_ref,
    second_ref,
    query_ref,
    output_ref,
    key_ref,
    value_ref,
    first_all,
    second_all,
    head_query,
    head_output,
    head_key,
    head_value,
    own_buf,
    head_buf,
    kv_buf,
    send_sem,
    recv_sem,
    own_sem,
    head_send,
    head_recv,
    head_own,
):
    group = lax.axis_index("grp")
    place = lax.axis_index("inner")
    peers = cols * lines
    row_y, core = group // 2, group % 2
    line, col = place // cols, place % cols
    other_y, other_x = 1 - row_y, 1 - col
    core_peer = (row_y * 2 + 1 - core, place)
    x_peer = (group, line * cols + other_x)
    y_peer = (other_y * 2 + core, place)
    arrays = ((first_ref, first_all), (second_ref, second_all))
    tokens = first_ref.shape[0]
    head_width = head_query.shape[1]
    kv_width = head_key.shape[1]
    share = peers // (key_ref.shape[1] // kv_width)

    def block(y, z, x, c=None):
        return ((y * 2 + (core if c is None else c)) * peers) + z * cols + x

    def inner_copies(to, slot, source, target):
        columns = pl.ds(pl.multiple_of(to * head_width, head_width), head_width)
        kv_columns = pl.ds(pl.multiple_of((to // share) * kv_width, kv_width), kv_width)
        rows = pl.ds(pl.multiple_of(source * tokens, tokens), tokens)
        pairs = (
            (query_ref.at[:, columns], head_query.at[rows]),
            (output_ref.at[:, columns], head_output.at[rows]),
            (key_ref.at[:, kv_columns], head_key.at[rows]),
            (value_ref.at[:, kv_columns], head_value.at[rows]),
        )
        return [
            pltpu.make_async_remote_copy(
                src_ref=src,
                dst_ref=dst,
                send_sem=head_send.at[number, slot],
                recv_sem=head_recv.at[number, slot],
                device_id=(group, target),
                device_id_type=MESH_ID,
            )
            for number, (src, dst) in enumerate(pairs)
        ]

    barrier = pltpu.get_barrier_semaphore()
    for step in range(1, peers):
        pl.semaphore_signal(
            barrier, inc=1, device_id=(group, lax.rem(place + step, peers)), device_id_type=MESH_ID
        )
    for peer in (core_peer, y_peer):
        pl.semaphore_signal(barrier, inc=1, device_id=peer, device_id_type=MESH_ID)
    pl.semaphore_wait(barrier, peers + 1)

    def copy(which, index, way, peer, own):
        source, gathered = arrays[which]
        return pltpu.make_async_remote_copy(
            src_ref=source if own else gathered.at[index],
            dst_ref=gathered.at[index],
            send_sem=send_sem.at[which, way, index],
            recv_sem=recv_sem.at[which, index],
            device_id=peer,
            device_id_type=MESH_ID,
        )

    def arrived(which, index):
        copy(which, index, 0, core_peer, False).wait_recv()

    UP, DOWN, XWAY, YWAY, CORE = range(5)
    sent = []

    def send(which, index, way, peer, own=False):
        copy(which, index, way, peer, own).start()

    def z_peer(delta):
        return (group, jnp.clip(line + delta, 0, lines - 1) * cols + col)

    own_index = block(row_y, line, col)
    local_in = [
        pltpu.make_async_copy(arrays[w][0], own_buf.at[w], own_sem.at[w]) for w in range(2)
    ]
    own_columns = pl.ds(pl.multiple_of(place * head_width, head_width), head_width)
    own_kv = pl.ds(pl.multiple_of((place // share) * kv_width, kv_width), kv_width)
    own_rows = pl.ds(pl.multiple_of(place * tokens, tokens), tokens)
    local_in += [
        pltpu.make_async_copy(query_ref.at[:, own_columns], head_buf.at[0], head_own.at[0]),
        pltpu.make_async_copy(output_ref.at[:, own_columns], head_buf.at[1], head_own.at[1]),
        pltpu.make_async_copy(key_ref.at[:, own_kv], kv_buf.at[0], head_own.at[2]),
        pltpu.make_async_copy(value_ref.at[:, own_kv], kv_buf.at[1], head_own.at[3]),
    ]
    local_out = [
        pltpu.make_async_copy(own_buf.at[w], arrays[w][1].at[own_index], own_sem.at[2 + w])
        for w in range(2)
    ]
    local_out += [
        pltpu.make_async_copy(head_buf.at[0], head_query.at[own_rows], head_own.at[4]),
        pltpu.make_async_copy(head_buf.at[1], head_output.at[own_rows], head_own.at[5]),
        pltpu.make_async_copy(kv_buf.at[0], head_key.at[own_rows], head_own.at[6]),
        pltpu.make_async_copy(kv_buf.at[1], head_value.at[own_rows], head_own.at[7]),
    ]

    def from_line(index, own, up, down):
        if up is not None:
            for w in range(2):

                @pl.when(up)
                def _():
                    send(w, index, UP, z_peer(1), own)

        if down is not None:
            for w in range(2):

                @pl.when(down)
                def _():
                    send(w, index, DOWN, z_peer(-1), own)

        send(0, index, XWAY, x_peer, own)
        send(1, index, YWAY, y_peer, own)
        send(1, index, XWAY, x_peer, own)
        send(0, index, YWAY, y_peer, own)
        for w in range(2):
            send(w, index, CORE, core_peer, own)

    def from_plane(z):
        index = block(row_y, z, other_x)
        arrived(0, index)
        send(0, index, YWAY, y_peer)
        send(0, index, CORE, core_peer)
        index = block(other_y, z, col)
        arrived(1, index)
        send(1, index, XWAY, x_peer)
        send(1, index, CORE, core_peer)

    def last_plane(z):
        for w, index in (
            (1, block(row_y, z, other_x)),
            (0, block(other_y, z, col)),
            (0, block(other_y, z, other_x)),
            (1, block(other_y, z, other_x)),
        ):
            arrived(w, index)
            send(w, index, CORE, core_peer)

    def at_distance(distance, act):
        for sign in (-1, 1):
            z = line + sign * distance

            @pl.when((z >= 0) & (z < lines))
            def _():
                act(z, sign)

    from_line(own_index, True, line < lines - 1, line > 0)
    for c in local_in:
        c.start()

    def head_start():
        for step in range(1, peers):
            to = lax.rem(place + step, peers)
            for c in inner_copies(to, step, place, to):
                c.start()

    for distance in range(lines):
        if distance:

            def take(z, sign):
                index = block(row_y, z, col)
                for w in range(2):
                    arrived(w, index)
                up = (line < lines - 1) if sign < 0 else None
                down = (line > 0) if sign > 0 else None
                from_line(index, False, up, down)

            at_distance(distance, take)
        if distance == max(0, lines - 2):
            head_start()
        if distance == 0:
            from_plane(line)
            for c in local_in:
                c.wait()
            for c in local_out:
                c.start()
        else:
            at_distance(distance, lambda z, sign: from_plane(z))

    last_plane(line)
    for distance in range(1, lines):
        at_distance(distance, lambda z, sign: last_plane(z))

    for y in range(2):
        for z in range(lines):
            for x in range(cols):
                for w in range(2):
                    arrived(w, block(y, z, x, 1 - core))
    for step in range(1, peers):
        source = lax.rem(place + peers - step, peers)
        for c in inner_copies(place, step, source, source):
            c.wait_recv()
        for c in inner_copies(lax.rem(place + step, peers), step, place, source):
            c.wait_send()
    for c in local_out:
        c.wait()

    def sent_wait(which, index, way):
        copy(which, index, way, core_peer, False).wait_send()

    for z in range(lines):
        index = block(row_y, z, col)
        for w in range(2):
            for way in (XWAY, YWAY):
                sent_wait(w, index, way)

            @pl.when((z <= line) & (line < lines - 1))
            def _():
                sent_wait(w, index, UP)

            @pl.when((z >= line) & (line > 0))
            def _():
                sent_wait(w, index, DOWN)

        sent_wait(0, block(row_y, z, other_x), YWAY)
        sent_wait(1, block(other_y, z, col), XWAY)
        for y in range(2):
            for x in range(cols):
                for w in range(2):
                    sent_wait(w, block(y, z, x), CORE)


def spread(first, second, queries, attn_out, keys, values, devices, peers, cols):
    tokens, width = first.shape
    head_width = queries.shape[1] // peers
    any_space = pl.BlockSpec(memory_space=pl.ANY)
    kind = first.dtype
    shapes = (
        jax.ShapeDtypeStruct((devices, tokens, width), kind),
        jax.ShapeDtypeStruct((devices, tokens, width), kind),
        jax.ShapeDtypeStruct((peers * tokens, head_width), kind),
        jax.ShapeDtypeStruct((peers * tokens, head_width), kind),
        jax.ShapeDtypeStruct((peers * tokens, HEAD_SIZE), kind),
        jax.ShapeDtypeStruct((peers * tokens, HEAD_SIZE), kind),
    )
    return pl.pallas_call(
        functools.partial(spread_kernel, cols, peers // cols),
        out_shape=shapes,
        in_specs=[any_space] * 6,
        out_specs=[any_space] * 6,
        scratch_shapes=[
            pltpu.VMEM((2, tokens, width), kind),
            pltpu.VMEM((2, tokens, head_width), kind),
            pltpu.VMEM((2, tokens, HEAD_SIZE), kind),
            pltpu.SemaphoreType.DMA((2, 5, devices)),
            pltpu.SemaphoreType.DMA((2, devices)),
            pltpu.SemaphoreType.DMA((4,)),
            pltpu.SemaphoreType.DMA((4, peers)),
            pltpu.SemaphoreType.DMA((4, peers)),
            pltpu.SemaphoreType.DMA((8,)),
        ],
        compiler_params=pltpu.CompilerParams(
            collective_id=0, has_side_effects=True, vmem_limit_bytes=8 * 2**20
        ),
        cost_estimate=pl.CostEstimate(
            flops=0, bytes_accessed=500 * 2**20, transcendentals=0
        ),
    )(first, second, queries, attn_out, keys, values)


def slot_ranks(named):
    tokens = named.shape[1]
    before = jnp.triu(jnp.ones((tokens, tokens), jnp.bfloat16), 1)
    return jnp.dot(named.astype(jnp.bfloat16), before, preferred_element_type=jnp.float32).astype(
        jnp.int32
    )


def per_device(
    grad_out,
    hidden,
    norm_gain,
    expert_ids,
    gate_weights,
    w_gate,
    w_up,
    w_down,
    w_out,
    queries,
    keys,
    values,
    attn_out,
    lse,
):
    token_rows, width = hidden.shape
    topk = expert_ids.shape[1]
    groups = lax.axis_size("grp")
    inner_product = lax.axis_size("inner")
    experts_all = w_gate.shape[0] * groups * inner_product
    capacity = max(2, 5 * token_rows * topk // (4 * experts_all))
    hidden_f = hidden.astype(jnp.float32)
    inverse = lax.rsqrt(jnp.mean(hidden_f * hidden_f, axis=1, keepdims=True) + EPSILON)
    normed = (hidden_f * inverse * norm_gain).astype(jnp.bfloat16)
    upstream = grad_out.astype(jnp.float32)
    cols = groups // 2
    devices = groups * inner_product
    gather_plan = (
        cols == 2
        and inner_product % cols == 0
        and w_gate.shape[0] == 1
        and 2 * devices * hidden.size * hidden.dtype.itemsize <= GATHER_LIMIT
    )
    if gather_plan:
        meta = jnp.concatenate(
            [expert_ids.astype(jnp.float32).T, gate_weights.T], axis=0
        )
        meta_all = lax.all_gather(meta, ("grp", "inner"), axis=0, tiled=True).reshape(
            devices, 2, topk, token_rows
        )
        normed_all, upstream_all, head_query, head_output, head_key, head_value = spread(
            normed, grad_out, queries, attn_out, keys, values, devices, inner_product, cols
        )
        expert = lax.axis_index("grp") * inner_product + lax.axis_index("inner")
        chosen = meta_all[:, 0].astype(jnp.int32) == expert
        named = jnp.any(chosen, axis=1)
        weight = jnp.sum(jnp.where(chosen, meta_all[:, 1], 0.0), axis=1)
        pick = (
            jnp.arange(capacity, dtype=jnp.int32)[None, :, None] == slot_ranks(named)[:, None, :]
        ) & named[:, None, :]
        slot_weight = jnp.sum(jnp.where(pick, weight[:, None, :], 0.0), axis=2)
        pick = pick.astype(jnp.bfloat16)
        slot_inputs = jnp.einsum("dct,dtw->dcw", pick, normed_all)
        slot_grads = jnp.einsum(
            "dct,dtw->dcw", pick, upstream_all, preferred_element_type=jnp.float32
        )
        slot_grads = (slot_grads * slot_weight[:, :, None]).astype(jnp.bfloat16)
        returned = lax.all_to_all(
            expert_rows_grads(
                slot_inputs.reshape(-1, width), slot_grads.reshape(-1, width), w_gate[0], w_up[0], w_down[0]
            ),
            ("grp", "inner"),
            split_axis=0,
            concat_axis=0,
            tiled=True,
        )
        mine = jnp.any(
            expert_ids.T[None] == jnp.arange(experts_all, dtype=jnp.int32)[:, None, None], axis=1
        )
        place = (
            (
                jnp.arange(capacity, dtype=jnp.int32)[None, :, None]
                == slot_ranks(mine)[:, None, :]
            )
            & mine[:, None, :]
        ).astype(jnp.bfloat16)
        grad_normed = contract_first(
            place.reshape(experts_all * capacity, token_rows), returned
        )
    else:
        flat_count = token_rows * topk
        flat_ids = expert_ids.reshape(-1)
        one_hot = (flat_ids[:, None] == jnp.arange(experts_all, dtype=jnp.int32)[None, :]).astype(
            jnp.int32
        )
        slot_rank = jnp.sum((jnp.cumsum(one_hot, axis=0) - one_hot) * one_hot, axis=1)
        target = flat_ids * capacity + slot_rank
        owner = (
            jnp.full((experts_all * capacity,), flat_count, jnp.int32)
            .at[target]
            .set(jnp.arange(flat_count, dtype=jnp.int32))
        )
        source_tok = owner // topk
        scaled = (
            (upstream[:, None, :] * gate_weights[:, :, None])
            .reshape(flat_count, width)
            .astype(jnp.bfloat16)
        )
        zero_row = jnp.zeros((1, width), jnp.bfloat16)
        slot_inputs = jnp.concatenate([normed, zero_row], axis=0)[source_tok]
        slot_grads = jnp.concatenate([scaled, zero_row], axis=0)[owner]
        outgoing = jnp.concatenate([slot_inputs, slot_grads], axis=1).reshape(
            experts_all, capacity, 2 * width
        )
        returned = lax.all_to_all(
            expert_grads(
                lax.all_to_all(outgoing, ("grp", "inner"), split_axis=0, concat_axis=0, tiled=True),
                w_gate,
                w_up,
                w_down,
            ),
            ("grp", "inner"),
            split_axis=0,
            concat_axis=0,
            tiled=True,
        )
        expert_rows = returned.reshape(-1, width)[target].astype(jnp.float32)
        grad_normed = jnp.sum(expert_rows.reshape(token_rows, topk, width), axis=1)
    gained = grad_normed * norm_gain
    statistic = jnp.mean(gained * hidden_f, axis=1, keepdims=True)
    grad_resid = (
        upstream + inverse * gained - hidden_f * inverse * inverse * inverse * statistic
    ).astype(jnp.bfloat16)
    head_width = queries.shape[1] // inner_product
    per_head = head_width // HEAD_SIZE
    shared_portion = inner_product // KEY_VALUE_HEADS
    if not gather_plan:
        key_value_pairs = jnp.concatenate(
            [
                keys.reshape(token_rows, KEY_VALUE_HEADS, 1, HEAD_SIZE),
                values.reshape(token_rows, KEY_VALUE_HEADS, 1, HEAD_SIZE),
            ],
            axis=2,
        )
        key_value_broadcast = jnp.broadcast_to(
            key_value_pairs[:, :, None], (token_rows, KEY_VALUE_HEADS, shared_portion, 2, HEAD_SIZE)
        ).reshape(token_rows, inner_product * 2 * HEAD_SIZE)
        head_query, head_output, head_kv = (
            lax.all_to_all(queries, "inner", split_axis=1, concat_axis=0, tiled=True),
            lax.all_to_all(attn_out, "inner", split_axis=1, concat_axis=0, tiled=True),
            lax.all_to_all(key_value_broadcast, "inner", split_axis=1, concat_axis=0, tiled=True),
        )
    head_grad = contract_last(
        lax.all_gather(grad_resid, "inner", axis=0, tiled=True), w_out
    ).astype(jnp.bfloat16)
    seq_len = head_query.shape[0]
    if not gather_plan:
        head_key = head_kv[:, :HEAD_SIZE]
        head_value = head_kv[:, HEAD_SIZE:]
    lse_rows = lse.T
    scale = float(HEAD_SIZE) ** (-0.5)
    blocks = 1
    while blocks < 8 and seq_len % (2 * blocks) == 0 and (seq_len // (2 * blocks) >= 512):
        blocks = blocks * 2
    block_len = seq_len // blocks
    grad_key_acc = jnp.zeros((seq_len, HEAD_SIZE), jnp.float32)
    grad_value_acc = jnp.zeros((seq_len, HEAD_SIZE), jnp.float32)
    query_parts = []
    for block_index in range(blocks):
        low = block_index * block_len
        high = low + block_len
        block_query = head_query[low:high].reshape(block_len * per_head, HEAD_SIZE)
        block_output = head_output[low:high].reshape(block_len * per_head, HEAD_SIZE)
        block_grad = head_grad[low:high].reshape(block_len * per_head, HEAD_SIZE)
        block_lse = lse_rows[low:high].reshape(-1)
        seen_key = head_key[:high]
        seen_value = head_value[:high]
        scores = contract_last(block_query, seen_key) * scale
        row_position = low + jnp.arange(block_len * per_head, dtype=jnp.int32) // per_head
        visible = jnp.arange(high, dtype=jnp.int32)[None, :] <= row_position[:, None]
        probs = jnp.where(visible, jnp.exp(scores - block_lse[:, None]), 0.0)
        grad_probs = contract_last(block_grad, seen_value)
        delta = jnp.sum(
            block_grad.astype(jnp.float32) * block_output.astype(jnp.float32), axis=1, keepdims=True
        )
        grad_scores = (probs * (grad_probs - delta)).astype(jnp.bfloat16)
        query_part = jnp.dot(grad_scores, seen_key, preferred_element_type=jnp.float32) * scale
        query_parts.append(query_part.reshape(block_len, head_width))
        grad_key_acc = grad_key_acc.at[:high].add(contract_first(grad_scores, block_query) * scale)
        grad_value_acc = grad_value_acc.at[:high].add(
            contract_first(probs.astype(jnp.bfloat16), block_grad)
        )
    grad_query_heads = jnp.concatenate(query_parts, axis=0)
    kv_heads = jnp.concatenate([grad_key_acc, grad_value_acc], axis=1)
    token_query, token_key_value = (
        lax.all_to_all(
            grad_query_heads.astype(jnp.bfloat16), "inner", split_axis=0, concat_axis=1, tiled=True
        ).astype(grad_query_heads.dtype),
        lax.all_to_all(
            kv_heads.astype(jnp.bfloat16), "inner", split_axis=0, concat_axis=1, tiled=True
        ).astype(kv_heads.dtype),
    )
    summed_total = jnp.sum(
        token_key_value.reshape(token_rows, KEY_VALUE_HEADS, shared_portion, 2, HEAD_SIZE), axis=2
    )
    keys_gradient = (
        summed_total[:, :, 0].reshape(token_rows, KEY_VALUE_HEADS * HEAD_SIZE).astype(jnp.bfloat16)
    )
    values_gradient = (
        summed_total[:, :, 1].reshape(token_rows, KEY_VALUE_HEADS * HEAD_SIZE).astype(jnp.bfloat16)
    )
    return (grad_resid, token_query.astype(jnp.bfloat16), keys_gradient, values_gradient)


def solution(mesh):
    placed = (
        P(("grp", "inner"), None),
        P(("grp", "inner"), None),
        P(),
        P(("grp", "inner"), None),
        P(("grp", "inner"), None),
        P(("grp", "inner"), None, None),
        P(("grp", "inner"), None, None),
        P(("grp", "inner"), None, None),
        P("inner", None),
        P(("grp", "inner"), None),
        P(("grp", "inner"), None),
        P(("grp", "inner"), None),
        P(("grp", "inner"), None),
        P("inner", "grp"),
    )
    return jax.shard_map(
        per_device,
        mesh=mesh,
        in_specs=placed,
        out_specs=(
            P(("grp", "inner"), None),
            P(("grp", "inner"), None),
            P(("grp", "inner"), None),
            P(("grp", "inner"), None),
        ),
        check_vma=False,
    )
```

```python
import functools

import jax
import jax.numpy as jnp
from jax import lax
from jax.experimental import pallas as pl
from jax.experimental.pallas import tpu as pltpu
from jax.sharding import PartitionSpec as P

KEY_VALUE_HEADS = 4
HEAD_SIZE = 128


EPSILON = 1e-06


def contract_last(left, right):
    return lax.dot_general(
        left, right, (((1,), (1,)), ((), ())), preferred_element_type=jnp.float32
    )


def contract_first(left, right):
    return lax.dot_general(
        left, right, (((0,), (0,)), ((), ())), preferred_element_type=jnp.float32
    )


def expert_rows_grads(inputs, upstream, gate_matrix, up_matrix, down_matrix):
    gate_pre = jnp.dot(inputs, gate_matrix, preferred_element_type=jnp.float32)
    up_pre = jnp.dot(inputs, up_matrix, preferred_element_type=jnp.float32)
    back_hidden = contract_last(upstream, down_matrix)
    sigmoid = jax.nn.sigmoid(gate_pre)
    grad_gate = (back_hidden * up_pre * sigmoid * (1.0 + gate_pre * (1.0 - sigmoid))).astype(
        jnp.bfloat16
    )
    grad_up = (back_hidden * gate_pre * sigmoid).astype(jnp.bfloat16)
    grad_in = contract_last(grad_gate, gate_matrix) + contract_last(grad_up, up_matrix)
    return grad_in.astype(jnp.bfloat16)


def expert_grads(received, w_gate, w_up, w_down):
    local = w_gate.shape[0]
    width = w_gate.shape[1]
    shaped = received.reshape((-1, local) + received.shape[1:])
    inputs = shaped[..., :width]
    upstream = shaped[..., width:]
    gate_pre = jnp.einsum("nlcd,ldf->nlcf", inputs, w_gate, preferred_element_type=jnp.float32)
    up_pre = jnp.einsum("nlcd,ldf->nlcf", inputs, w_up, preferred_element_type=jnp.float32)
    back_hidden = jnp.einsum("nlcd,lfd->nlcf", upstream, w_down, preferred_element_type=jnp.float32)
    sigmoid = jax.nn.sigmoid(gate_pre)
    grad_gate = (back_hidden * up_pre * sigmoid * (1.0 + gate_pre * (1.0 - sigmoid))).astype(
        jnp.bfloat16
    )
    grad_up = (back_hidden * gate_pre * sigmoid).astype(jnp.bfloat16)
    grad_in = jnp.einsum("nlcf,ldf->nlcd", grad_gate, w_gate, preferred_element_type=jnp.float32)
    grad_in = grad_in + jnp.einsum(
        "nlcf,ldf->nlcd", grad_up, w_up, preferred_element_type=jnp.float32
    )
    return grad_in.astype(jnp.bfloat16).reshape(received.shape[:-1] + (width,))


MESH_ID = pl.DeviceIdType.MESH
GATHER_LIMIT = 48 * 2**20


def spread_kernel(
    cols,
    lines,
    first_ref,
    second_ref,
    query_ref,
    output_ref,
    key_ref,
    value_ref,
    first_all,
    second_all,
    head_query,
    head_output,
    head_key,
    head_value,
    own_first,
    own_second,
    head_buf,
    kv_buf,
    send_sem,
    recv_sem,
    own_sem,
    head_send,
    head_recv,
    head_own,
):
    group = lax.axis_index("grp")
    place = lax.axis_index("inner")
    peers = cols * lines
    row_y, core = group // 2, group % 2
    line, col = place // cols, place % cols
    other_y, other_x = 1 - row_y, 1 - col
    core_peer = (row_y * 2 + 1 - core, place)
    x_peer = (group, line * cols + other_x)
    y_peer = (other_y * 2 + core, place)
    arrays = ((first_ref, first_all), (second_ref, second_all))
    own_bufs = (own_first, own_second)
    tokens = first_ref.shape[0]
    head_width = head_query.shape[1]
    kv_width = head_key.shape[1]
    share = peers // (key_ref.shape[1] // kv_width)

    def block(y, z, x, c=None):
        return ((y * 2 + (core if c is None else c)) * peers) + z * cols + x

    def inner_copies(to, slot, source, target):
        columns = pl.ds(pl.multiple_of(to * head_width, head_width), head_width)
        kv_columns = pl.ds(pl.multiple_of((to // share) * kv_width, kv_width), kv_width)
        rows = pl.ds(pl.multiple_of(source * tokens, tokens), tokens)
        pairs = (
            (query_ref.at[:, columns], head_query.at[rows]),
            (output_ref.at[:, columns], head_output.at[rows]),
            (key_ref.at[:, kv_columns], head_key.at[rows]),
            (value_ref.at[:, kv_columns], head_value.at[rows]),
        )
        return [
            pltpu.make_async_remote_copy(
                src_ref=src,
                dst_ref=dst,
                send_sem=head_send.at[number, slot],
                recv_sem=head_recv.at[number, slot],
                device_id=(group, target),
                device_id_type=MESH_ID,
            )
            for number, (src, dst) in enumerate(pairs)
        ]

    barrier = pltpu.get_barrier_semaphore()
    for step in range(1, peers):
        pl.semaphore_signal(
            barrier, inc=1, device_id=(group, lax.rem(place + step, peers)), device_id_type=MESH_ID
        )
    for peer in (core_peer, y_peer):
        pl.semaphore_signal(barrier, inc=1, device_id=peer, device_id_type=MESH_ID)
    pl.semaphore_wait(barrier, peers + 1)

    def copy(which, index, way, peer, own):
        source, gathered = arrays[which]
        return pltpu.make_async_remote_copy(
            src_ref=source if own else gathered.at[index],
            dst_ref=gathered.at[index],
            send_sem=send_sem.at[which, way, index],
            recv_sem=recv_sem.at[which, index],
            device_id=peer,
            device_id_type=MESH_ID,
        )

    def arrived(which, index):
        copy(which, index, 0, core_peer, False).wait_recv()

    UP, DOWN, XWAY, YWAY, CORE = range(5)
    sent = []

    def send(which, index, way, peer, own=False):
        copy(which, index, way, peer, own).start()

    def z_peer(delta):
        return (group, jnp.clip(line + delta, 0, lines - 1) * cols + col)

    own_index = block(row_y, line, col)
    local_in = [
        pltpu.make_async_copy(arrays[w][0], own_bufs[w], own_sem.at[w]) for w in range(2)
    ]
    own_columns = pl.ds(pl.multiple_of(place * head_width, head_width), head_width)
    own_kv = pl.ds(pl.multiple_of((place // share) * kv_width, kv_width), kv_width)
    own_rows = pl.ds(pl.multiple_of(place * tokens, tokens), tokens)
    local_in += [
        pltpu.make_async_copy(query_ref.at[:, own_columns], head_buf.at[0], head_own.at[0]),
        pltpu.make_async_copy(output_ref.at[:, own_columns], head_buf.at[1], head_own.at[1]),
        pltpu.make_async_copy(key_ref.at[:, own_kv], kv_buf.at[0], head_own.at[2]),
        pltpu.make_async_copy(value_ref.at[:, own_kv], kv_buf.at[1], head_own.at[3]),
    ]
    local_out = [
        pltpu.make_async_copy(own_bufs[w], arrays[w][1].at[own_index], own_sem.at[2 + w])
        for w in range(2)
    ]
    local_out += [
        pltpu.make_async_copy(head_buf.at[0], head_query.at[own_rows], head_own.at[4]),
        pltpu.make_async_copy(head_buf.at[1], head_output.at[own_rows], head_own.at[5]),
        pltpu.make_async_copy(kv_buf.at[0], head_key.at[own_rows], head_own.at[6]),
        pltpu.make_async_copy(kv_buf.at[1], head_value.at[own_rows], head_own.at[7]),
    ]

    def from_line(index, own, up, down):
        if up is not None:
            for w in range(2):

                @pl.when(up)
                def _():
                    send(w, index, UP, z_peer(1), own)

        if down is not None:
            for w in range(2):

                @pl.when(down)
                def _():
                    send(w, index, DOWN, z_peer(-1), own)

        send(0, index, XWAY, x_peer, own)
        send(1, index, YWAY, y_peer, own)
        send(1, index, XWAY, x_peer, own)
        send(0, index, YWAY, y_peer, own)
        for w in range(2):
            send(w, index, CORE, core_peer, own)

    def from_plane(z):
        index = block(row_y, z, other_x)
        arrived(0, index)
        send(0, index, YWAY, y_peer)
        send(0, index, CORE, core_peer)
        index = block(other_y, z, col)
        arrived(1, index)
        send(1, index, XWAY, x_peer)
        send(1, index, CORE, core_peer)

    def last_plane(z):
        for w, index in (
            (1, block(row_y, z, other_x)),
            (0, block(other_y, z, col)),
            (0, block(other_y, z, other_x)),
            (1, block(other_y, z, other_x)),
        ):
            arrived(w, index)
            send(w, index, CORE, core_peer)

    def at_distance(distance, act):
        for sign in (-1, 1):
            z = line + sign * distance

            @pl.when((z >= 0) & (z < lines))
            def _():
                act(z, sign)

    from_line(own_index, True, line < lines - 1, line > 0)
    for c in local_in:
        c.start()

    def head_start():
        for step in range(1, peers):
            to = lax.rem(place + step, peers)
            for c in inner_copies(to, step, place, to):
                c.start()

    for distance in range(lines):
        if distance:

            def take(z, sign):
                index = block(row_y, z, col)
                for w in range(2):
                    arrived(w, index)
                up = (line < lines - 1) if sign < 0 else None
                down = (line > 0) if sign > 0 else None
                from_line(index, False, up, down)

            at_distance(distance, take)
        if distance == max(0, lines - 2):
            head_start()
        if distance == 0:
            from_plane(line)
            for c in local_in:
                c.wait()
            for c in local_out:
                c.start()
        else:
            at_distance(distance, lambda z, sign: from_plane(z))

    last_plane(line)
    for distance in range(1, lines):
        at_distance(distance, lambda z, sign: last_plane(z))

    for y in range(2):
        for z in range(lines):
            for x in range(cols):
                for w in range(2):
                    arrived(w, block(y, z, x, 1 - core))
    for step in range(1, peers):
        source = lax.rem(place + peers - step, peers)
        for c in inner_copies(place, step, source, source):
            c.wait_recv()
        for c in inner_copies(lax.rem(place + step, peers), step, place, source):
            c.wait_send()
    for c in local_out:
        c.wait()

    def sent_wait(which, index, way):
        copy(which, index, way, core_peer, False).wait_send()

    for z in range(lines):
        index = block(row_y, z, col)
        for w in range(2):
            for way in (XWAY, YWAY):
                sent_wait(w, index, way)

            @pl.when((z <= line) & (line < lines - 1))
            def _():
                sent_wait(w, index, UP)

            @pl.when((z >= line) & (line > 0))
            def _():
                sent_wait(w, index, DOWN)

        sent_wait(0, block(row_y, z, other_x), YWAY)
        sent_wait(1, block(other_y, z, col), XWAY)
        for y in range(2):
            for x in range(cols):
                for w in range(2):
                    sent_wait(w, block(y, z, x), CORE)


def spread(first, second, queries, attn_out, keys, values, devices, peers, cols):
    tokens = first.shape[0]
    head_width = queries.shape[1] // peers
    any_space = pl.BlockSpec(memory_space=pl.ANY)
    kind = first.dtype
    shapes = (
        jax.ShapeDtypeStruct((devices,) + first.shape, kind),
        jax.ShapeDtypeStruct((devices,) + second.shape, kind),
        jax.ShapeDtypeStruct((peers * tokens, head_width), kind),
        jax.ShapeDtypeStruct((peers * tokens, head_width), kind),
        jax.ShapeDtypeStruct((peers * tokens, HEAD_SIZE), kind),
        jax.ShapeDtypeStruct((peers * tokens, HEAD_SIZE), kind),
    )
    return pl.pallas_call(
        functools.partial(spread_kernel, cols, peers // cols),
        out_shape=shapes,
        in_specs=[any_space] * 6,
        out_specs=[any_space] * 6,
        scratch_shapes=[
            pltpu.VMEM(first.shape, kind),
            pltpu.VMEM(second.shape, kind),
            pltpu.VMEM((2, tokens, head_width), kind),
            pltpu.VMEM((2, tokens, HEAD_SIZE), kind),
            pltpu.SemaphoreType.DMA((2, 5, devices)),
            pltpu.SemaphoreType.DMA((2, devices)),
            pltpu.SemaphoreType.DMA((4,)),
            pltpu.SemaphoreType.DMA((4, peers)),
            pltpu.SemaphoreType.DMA((4, peers)),
            pltpu.SemaphoreType.DMA((8,)),
        ],
        compiler_params=pltpu.CompilerParams(
            collective_id=0, has_side_effects=True, vmem_limit_bytes=8 * 2**20
        ),
        cost_estimate=pl.CostEstimate(
            flops=0, bytes_accessed=500 * 2**20, transcendentals=0
        ),
    )(first, second, queries, attn_out, keys, values)


META_LANES = 128


def pick_kernel(expert_ref, first_ref, second_ref, inputs_ref, grads_ref):
    width = inputs_ref.shape[1]
    capacity = inputs_ref.shape[0]
    tokens, first_width = first_ref.shape
    topk = expert_ref[1]
    meta = first_ref[:, first_width - META_LANES :]
    lane = lax.broadcasted_iota(jnp.int32, (tokens, META_LANES), 1)
    chosen = jnp.where(
        (meta.astype(jnp.float32) == expert_ref[0].astype(jnp.float32)) & (lane < topk), 1.0, 0.0
    )
    source = lax.broadcasted_iota(jnp.int32, (META_LANES, META_LANES), 0)
    target = lax.broadcasted_iota(jnp.int32, (META_LANES, META_LANES), 1)
    away = source - target
    fold = (
        (target < topk) & ((away == topk) | (away == 2 * topk) | (away == 3 * topk))
    ).astype(jnp.float32).astype(jnp.bfloat16)
    gates = jnp.dot(meta, fold, preferred_element_type=jnp.float32)
    weight = jnp.sum(chosen * gates, axis=1, keepdims=True)
    named = contract_last(jnp.ones((8, META_LANES), jnp.bfloat16), chosen.astype(jnp.bfloat16))
    row = lax.broadcasted_iota(jnp.int32, (tokens, tokens), 0)
    column = lax.broadcasted_iota(jnp.int32, (tokens, tokens), 1)
    before = (row < column).astype(jnp.float32).astype(jnp.bfloat16)
    rank = jnp.dot(named.astype(jnp.bfloat16), before, preferred_element_type=jnp.float32)
    slot = lax.broadcasted_iota(jnp.int32, (capacity, tokens), 0).astype(jnp.float32)
    pick = jnp.where((slot == rank[:1]) & (named[:1] > 0.5), 1.0, 0.0).astype(jnp.bfloat16)

    def picked(rows):
        return jnp.dot(pick, rows, preferred_element_type=jnp.float32).astype(jnp.bfloat16)

    def scaled(rows):
        return (rows.astype(jnp.float32) * weight).astype(jnp.bfloat16)

    extra = first_width - META_LANES - width
    inputs_ref[...] = picked(first_ref[:, :width])
    grads_ref[:, :extra] = picked(scaled(first_ref[:, width : width + extra]))
    grads_ref[:, extra:] = picked(scaled(second_ref[...]))


def pick_rows(expert, topk, first_all, second_all, capacity, width):
    devices, tokens, first_width = first_all.shape
    second_width = second_all.shape[2]
    out = jax.ShapeDtypeStruct((devices * capacity, width), first_all.dtype)
    return pl.pallas_call(
        pick_kernel,
        grid_spec=pltpu.PrefetchScalarGridSpec(
            num_scalar_prefetch=1,
            grid=(devices,),
            in_specs=[
                pl.BlockSpec((None, tokens, first_width), lambda d, e: (d, 0, 0)),
                pl.BlockSpec((None, tokens, second_width), lambda d, e: (d, 0, 0)),
            ],
            out_specs=[pl.BlockSpec((capacity, width), lambda d, e: (d, 0))] * 2,
        ),
        out_shape=(out, out),
        compiler_params=pltpu.CompilerParams(vmem_limit_bytes=24 * 2**20),
    )(jnp.stack([expert, jnp.int32(topk)]), first_all, second_all)


def slot_ranks(named):
    tokens = named.shape[1]
    before = jnp.triu(jnp.ones((tokens, tokens), jnp.bfloat16), 1)
    return jnp.dot(named.astype(jnp.bfloat16), before, preferred_element_type=jnp.float32).astype(
        jnp.int32
    )


def per_device(
    grad_out,
    hidden,
    norm_gain,
    expert_ids,
    gate_weights,
    w_gate,
    w_up,
    w_down,
    w_out,
    queries,
    keys,
    values,
    attn_out,
    lse,
):
    token_rows, width = hidden.shape
    topk = expert_ids.shape[1]
    groups = lax.axis_size("grp")
    inner_product = lax.axis_size("inner")
    experts_all = w_gate.shape[0] * groups * inner_product
    capacity = max(2, 5 * token_rows * topk // (4 * experts_all))
    hidden_f = hidden.astype(jnp.float32)
    inverse = lax.rsqrt(jnp.mean(hidden_f * hidden_f, axis=1, keepdims=True) + EPSILON)
    normed = (hidden_f * inverse * norm_gain).astype(jnp.bfloat16)
    upstream = grad_out.astype(jnp.float32)
    cols = groups // 2
    devices = groups * inner_product
    gather_plan = (
        cols == 2
        and inner_product % cols == 0
        and w_gate.shape[0] == 1
        and experts_all <= 256
        and 4 * topk <= META_LANES
        and 2 * devices * hidden.size * hidden.dtype.itemsize <= GATHER_LIMIT
    )
    if gather_plan:
        high = lax.reduce_precision(gate_weights, 8, 7)
        middle = lax.reduce_precision(gate_weights - high, 8, 7)
        low = gate_weights - high - middle
        extra = width // 4
        blank = jnp.zeros((token_rows, META_LANES - 4 * topk), jnp.bfloat16)
        first = jnp.concatenate(
            [
                normed,
                grad_out[:, :extra],
                expert_ids.astype(jnp.bfloat16),
                high.astype(jnp.bfloat16),
                middle.astype(jnp.bfloat16),
                low.astype(jnp.bfloat16),
                blank,
            ],
            axis=1,
        )
        first_all, second_all, head_query, head_output, head_key, head_value = spread(
            first,
            grad_out[:, extra:],
            queries,
            attn_out,
            keys,
            values,
            devices,
            inner_product,
            cols,
        )
        expert = lax.axis_index("grp") * inner_product + lax.axis_index("inner")
        slot_inputs, slot_grads = pick_rows(
            expert, topk, first_all, second_all, capacity, width
        )
        returned = lax.all_to_all(
            expert_rows_grads(
                slot_inputs, slot_grads, w_gate[0], w_up[0], w_down[0]
            ),
            ("grp", "inner"),
            split_axis=0,
            concat_axis=0,
            tiled=True,
        )
        mine = jnp.any(
            expert_ids.T[None] == jnp.arange(experts_all, dtype=jnp.int32)[:, None, None], axis=1
        )
        place = (
            (
                jnp.arange(capacity, dtype=jnp.int32)[None, :, None]
                == slot_ranks(mine)[:, None, :]
            )
            & mine[:, None, :]
        ).astype(jnp.bfloat16)
        grad_normed = contract_first(
            place.reshape(experts_all * capacity, token_rows), returned
        )
    else:
        flat_count = token_rows * topk
        flat_ids = expert_ids.reshape(-1)
        one_hot = (flat_ids[:, None] == jnp.arange(experts_all, dtype=jnp.int32)[None, :]).astype(
            jnp.int32
        )
        slot_rank = jnp.sum((jnp.cumsum(one_hot, axis=0) - one_hot) * one_hot, axis=1)
        target = flat_ids * capacity + slot_rank
        owner = (
            jnp.full((experts_all * capacity,), flat_count, jnp.int32)
            .at[target]
            .set(jnp.arange(flat_count, dtype=jnp.int32))
        )
        source_tok = owner // topk
        scaled = (
            (upstream[:, None, :] * gate_weights[:, :, None])
            .reshape(flat_count, width)
            .astype(jnp.bfloat16)
        )
        zero_row = jnp.zeros((1, width), jnp.bfloat16)
        slot_inputs = jnp.concatenate([normed, zero_row], axis=0)[source_tok]
        slot_grads = jnp.concatenate([scaled, zero_row], axis=0)[owner]
        outgoing = jnp.concatenate([slot_inputs, slot_grads], axis=1).reshape(
            experts_all, capacity, 2 * width
        )
        returned = lax.all_to_all(
            expert_grads(
                lax.all_to_all(outgoing, ("grp", "inner"), split_axis=0, concat_axis=0, tiled=True),
                w_gate,
                w_up,
                w_down,
            ),
            ("grp", "inner"),
            split_axis=0,
            concat_axis=0,
            tiled=True,
        )
        expert_rows = returned.reshape(-1, width)[target].astype(jnp.float32)
        grad_normed = jnp.sum(expert_rows.reshape(token_rows, topk, width), axis=1)
    gained = grad_normed * norm_gain
    statistic = jnp.mean(gained * hidden_f, axis=1, keepdims=True)
    grad_resid = (
        upstream + inverse * gained - hidden_f * inverse * inverse * inverse * statistic
    ).astype(jnp.bfloat16)
    head_width = queries.shape[1] // inner_product
    per_head = head_width // HEAD_SIZE
    shared_portion = inner_product // KEY_VALUE_HEADS
    if not gather_plan:
        key_value_pairs = jnp.concatenate(
            [
                keys.reshape(token_rows, KEY_VALUE_HEADS, 1, HEAD_SIZE),
                values.reshape(token_rows, KEY_VALUE_HEADS, 1, HEAD_SIZE),
            ],
            axis=2,
        )
        key_value_broadcast = jnp.broadcast_to(
            key_value_pairs[:, :, None], (token_rows, KEY_VALUE_HEADS, shared_portion, 2, HEAD_SIZE)
        ).reshape(token_rows, inner_product * 2 * HEAD_SIZE)
        head_query, head_output, head_kv = (
            lax.all_to_all(queries, "inner", split_axis=1, concat_axis=0, tiled=True),
            lax.all_to_all(attn_out, "inner", split_axis=1, concat_axis=0, tiled=True),
            lax.all_to_all(key_value_broadcast, "inner", split_axis=1, concat_axis=0, tiled=True),
        )
    head_grad = contract_last(
        lax.all_gather(grad_resid, "inner", axis=0, tiled=True), w_out
    ).astype(jnp.bfloat16)
    seq_len = head_query.shape[0]
    if not gather_plan:
        head_key = head_kv[:, :HEAD_SIZE]
        head_value = head_kv[:, HEAD_SIZE:]
    lse_rows = lse.T
    scale = float(HEAD_SIZE) ** (-0.5)
    blocks = 1
    while blocks < 8 and seq_len % (2 * blocks) == 0 and (seq_len // (2 * blocks) >= 512):
        blocks = blocks * 2
    block_len = seq_len // blocks
    grad_key_acc = jnp.zeros((seq_len, HEAD_SIZE), jnp.float32)
    grad_value_acc = jnp.zeros((seq_len, HEAD_SIZE), jnp.float32)
    query_parts = []
    for block_index in range(blocks):
        low = block_index * block_len
        high = low + block_len
        block_query = head_query[low:high].reshape(block_len * per_head, HEAD_SIZE)
        block_output = head_output[low:high].reshape(block_len * per_head, HEAD_SIZE)
        block_grad = head_grad[low:high].reshape(block_len * per_head, HEAD_SIZE)
        block_lse = lse_rows[low:high].reshape(-1)
        seen_key = head_key[:high]
        seen_value = head_value[:high]
        scores = contract_last(block_query, seen_key) * scale
        row_position = low + jnp.arange(block_len * per_head, dtype=jnp.int32) // per_head
        visible = jnp.arange(high, dtype=jnp.int32)[None, :] <= row_position[:, None]
        probs = jnp.where(visible, jnp.exp(scores - block_lse[:, None]), 0.0)
        grad_probs = contract_last(block_grad, seen_value)
        delta = jnp.sum(
            block_grad.astype(jnp.float32) * block_output.astype(jnp.float32), axis=1, keepdims=True
        )
        grad_scores = (probs * (grad_probs - delta)).astype(jnp.bfloat16)
        query_part = jnp.dot(grad_scores, seen_key, preferred_element_type=jnp.float32) * scale
        query_parts.append(query_part.reshape(block_len, head_width))
        grad_key_acc = grad_key_acc.at[:high].add(contract_first(grad_scores, block_query) * scale)
        grad_value_acc = grad_value_acc.at[:high].add(
            contract_first(probs.astype(jnp.bfloat16), block_grad)
        )
    grad_query_heads = jnp.concatenate(query_parts, axis=0)
    kv_heads = jnp.concatenate([grad_key_acc, grad_value_acc], axis=1)
    token_query, token_key_value = (
        lax.all_to_all(
            grad_query_heads.astype(jnp.bfloat16), "inner", split_axis=0, concat_axis=1, tiled=True
        ).astype(grad_query_heads.dtype),
        lax.all_to_all(
            kv_heads.astype(jnp.bfloat16), "inner", split_axis=0, concat_axis=1, tiled=True
        ).astype(kv_heads.dtype),
    )
    summed_total = jnp.sum(
        token_key_value.reshape(token_rows, KEY_VALUE_HEADS, shared_portion, 2, HEAD_SIZE), axis=2
    )
    keys_gradient = (
        summed_total[:, :, 0].reshape(token_rows, KEY_VALUE_HEADS * HEAD_SIZE).astype(jnp.bfloat16)
    )
    values_gradient = (
        summed_total[:, :, 1].reshape(token_rows, KEY_VALUE_HEADS * HEAD_SIZE).astype(jnp.bfloat16)
    )
    return (grad_resid, token_query.astype(jnp.bfloat16), keys_gradient, values_gradient)


def solution(mesh):
    placed = (
        P(("grp", "inner"), None),
        P(("grp", "inner"), None),
        P(),
        P(("grp", "inner"), None),
        P(("grp", "inner"), None),
        P(("grp", "inner"), None, None),
        P(("grp", "inner"), None, None),
        P(("grp", "inner"), None, None),
        P("inner", None),
        P(("grp", "inner"), None),
        P(("grp", "inner"), None),
        P(("grp", "inner"), None),
        P(("grp", "inner"), None),
        P("inner", "grp"),
    )
    return jax.shard_map(
        per_device,
        mesh=mesh,
        in_specs=placed,
        out_specs=(
            P(("grp", "inner"), None),
            P(("grp", "inner"), None),
            P(("grp", "inner"), None),
            P(("grp", "inner"), None),
        ),
        check_vma=False,
    )
```

```python
import functools

import jax
import jax.numpy as jnp
from jax import lax
from jax.experimental import pallas as pl
from jax.experimental.pallas import tpu as pltpu
from jax.sharding import PartitionSpec as P

KEY_VALUE_HEADS = 4
HEAD_SIZE = 128


EPSILON = 1e-06


def contract_last(left, right):
    return lax.dot_general(
        left, right, (((1,), (1,)), ((), ())), preferred_element_type=jnp.float32
    )


def contract_first(left, right):
    return lax.dot_general(
        left, right, (((0,), (0,)), ((), ())), preferred_element_type=jnp.float32
    )


def expert_rows_grads(inputs, upstream, gate_matrix, up_matrix, down_matrix):
    gate_pre = jnp.dot(inputs, gate_matrix, preferred_element_type=jnp.float32)
    up_pre = jnp.dot(inputs, up_matrix, preferred_element_type=jnp.float32)
    back_hidden = contract_last(upstream, down_matrix)
    sigmoid = jax.nn.sigmoid(gate_pre)
    grad_gate = (back_hidden * up_pre * sigmoid * (1.0 + gate_pre * (1.0 - sigmoid))).astype(
        jnp.bfloat16
    )
    grad_up = (back_hidden * gate_pre * sigmoid).astype(jnp.bfloat16)
    half = gate_matrix.shape[0] // 2

    def columns(gate_rows, up_rows):
        grad_in = contract_last(grad_gate, gate_rows) + contract_last(grad_up, up_rows)
        return grad_in.astype(jnp.bfloat16)

    first = columns(gate_matrix[:half], up_matrix[:half])
    return first, columns(gate_matrix[half:], up_matrix[half:])


def expert_grads(received, w_gate, w_up, w_down):
    local = w_gate.shape[0]
    width = w_gate.shape[1]
    shaped = received.reshape((-1, local) + received.shape[1:])
    inputs = shaped[..., :width]
    upstream = shaped[..., width:]
    gate_pre = jnp.einsum("nlcd,ldf->nlcf", inputs, w_gate, preferred_element_type=jnp.float32)
    up_pre = jnp.einsum("nlcd,ldf->nlcf", inputs, w_up, preferred_element_type=jnp.float32)
    back_hidden = jnp.einsum("nlcd,lfd->nlcf", upstream, w_down, preferred_element_type=jnp.float32)
    sigmoid = jax.nn.sigmoid(gate_pre)
    grad_gate = (back_hidden * up_pre * sigmoid * (1.0 + gate_pre * (1.0 - sigmoid))).astype(
        jnp.bfloat16
    )
    grad_up = (back_hidden * gate_pre * sigmoid).astype(jnp.bfloat16)
    grad_in = jnp.einsum("nlcf,ldf->nlcd", grad_gate, w_gate, preferred_element_type=jnp.float32)
    grad_in = grad_in + jnp.einsum(
        "nlcf,ldf->nlcd", grad_up, w_up, preferred_element_type=jnp.float32
    )
    return grad_in.astype(jnp.bfloat16).reshape(received.shape[:-1] + (width,))


MESH_ID = pl.DeviceIdType.MESH
GATHER_LIMIT = 48 * 2**20


def spread_kernel(
    cols,
    lines,
    first_ref,
    second_ref,
    query_ref,
    output_ref,
    key_ref,
    value_ref,
    first_all,
    second_all,
    head_query,
    head_output,
    head_key,
    head_value,
    own_first,
    own_second,
    head_buf,
    kv_buf,
    send_sem,
    recv_sem,
    own_sem,
    head_send,
    head_recv,
    head_own,
):
    group = lax.axis_index("grp")
    place = lax.axis_index("inner")
    peers = cols * lines
    row_y, core = group // 2, group % 2
    line, col = place // cols, place % cols
    other_y, other_x = 1 - row_y, 1 - col
    core_peer = (row_y * 2 + 1 - core, place)
    x_peer = (group, line * cols + other_x)
    y_peer = (other_y * 2 + core, place)
    arrays = ((first_ref, first_all), (second_ref, second_all))
    own_bufs = (own_first, own_second)
    tokens = first_ref.shape[0]
    head_width = head_query.shape[1]
    kv_width = head_key.shape[1]
    share = peers // (key_ref.shape[1] // kv_width)

    def block(y, z, x, c=None):
        return ((y * 2 + (core if c is None else c)) * peers) + z * cols + x

    def inner_copies(to, slot, source, target):
        columns = pl.ds(pl.multiple_of(to * head_width, head_width), head_width)
        kv_columns = pl.ds(pl.multiple_of((to // share) * kv_width, kv_width), kv_width)
        rows = pl.ds(pl.multiple_of(source * tokens, tokens), tokens)
        pairs = (
            (query_ref.at[:, columns], head_query.at[rows]),
            (output_ref.at[:, columns], head_output.at[rows]),
            (key_ref.at[:, kv_columns], head_key.at[rows]),
            (value_ref.at[:, kv_columns], head_value.at[rows]),
        )
        return [
            pltpu.make_async_remote_copy(
                src_ref=src,
                dst_ref=dst,
                send_sem=head_send.at[number, slot],
                recv_sem=head_recv.at[number, slot],
                device_id=(group, target),
                device_id_type=MESH_ID,
            )
            for number, (src, dst) in enumerate(pairs)
        ]

    barrier = pltpu.get_barrier_semaphore()
    for step in range(1, peers):
        pl.semaphore_signal(
            barrier, inc=1, device_id=(group, lax.rem(place + step, peers)), device_id_type=MESH_ID
        )
    for peer in (core_peer, y_peer):
        pl.semaphore_signal(barrier, inc=1, device_id=peer, device_id_type=MESH_ID)
    pl.semaphore_wait(barrier, peers + 1)

    def copy(which, index, way, peer, own):
        source, gathered = arrays[which]
        return pltpu.make_async_remote_copy(
            src_ref=source if own else gathered.at[index],
            dst_ref=gathered.at[index],
            send_sem=send_sem.at[which, way, index],
            recv_sem=recv_sem.at[which, index],
            device_id=peer,
            device_id_type=MESH_ID,
        )

    def arrived(which, index):
        copy(which, index, 0, core_peer, False).wait_recv()

    UP, DOWN, XWAY, YWAY, CORE = range(5)
    sent = []

    def send(which, index, way, peer, own=False):
        copy(which, index, way, peer, own).start()

    def z_peer(delta):
        return (group, jnp.clip(line + delta, 0, lines - 1) * cols + col)

    own_index = block(row_y, line, col)
    local_in = [
        pltpu.make_async_copy(arrays[w][0], own_bufs[w], own_sem.at[w]) for w in range(2)
    ]
    own_columns = pl.ds(pl.multiple_of(place * head_width, head_width), head_width)
    own_kv = pl.ds(pl.multiple_of((place // share) * kv_width, kv_width), kv_width)
    own_rows = pl.ds(pl.multiple_of(place * tokens, tokens), tokens)
    local_in += [
        pltpu.make_async_copy(query_ref.at[:, own_columns], head_buf.at[0], head_own.at[0]),
        pltpu.make_async_copy(output_ref.at[:, own_columns], head_buf.at[1], head_own.at[1]),
        pltpu.make_async_copy(key_ref.at[:, own_kv], kv_buf.at[0], head_own.at[2]),
        pltpu.make_async_copy(value_ref.at[:, own_kv], kv_buf.at[1], head_own.at[3]),
    ]
    local_out = [
        pltpu.make_async_copy(own_bufs[w], arrays[w][1].at[own_index], own_sem.at[2 + w])
        for w in range(2)
    ]
    local_out += [
        pltpu.make_async_copy(head_buf.at[0], head_query.at[own_rows], head_own.at[4]),
        pltpu.make_async_copy(head_buf.at[1], head_output.at[own_rows], head_own.at[5]),
        pltpu.make_async_copy(kv_buf.at[0], head_key.at[own_rows], head_own.at[6]),
        pltpu.make_async_copy(kv_buf.at[1], head_value.at[own_rows], head_own.at[7]),
    ]

    def from_line(index, own, up, down):
        if up is not None:
            for w in range(2):

                @pl.when(up)
                def _():
                    send(w, index, UP, z_peer(1), own)

        if down is not None:
            for w in range(2):

                @pl.when(down)
                def _():
                    send(w, index, DOWN, z_peer(-1), own)

        send(0, index, XWAY, x_peer, own)
        send(1, index, YWAY, y_peer, own)
        send(1, index, XWAY, x_peer, own)
        send(0, index, YWAY, y_peer, own)
        for w in range(2):
            send(w, index, CORE, core_peer, own)

    def from_plane(z):
        index = block(row_y, z, other_x)
        arrived(0, index)
        send(0, index, YWAY, y_peer)
        send(0, index, CORE, core_peer)
        index = block(other_y, z, col)
        arrived(1, index)
        send(1, index, XWAY, x_peer)
        send(1, index, CORE, core_peer)

    def last_plane(z):
        for w, index in (
            (1, block(row_y, z, other_x)),
            (0, block(other_y, z, col)),
            (0, block(other_y, z, other_x)),
            (1, block(other_y, z, other_x)),
        ):
            arrived(w, index)
            send(w, index, CORE, core_peer)

    def at_distance(distance, act):
        for sign in (-1, 1):
            z = line + sign * distance

            @pl.when((z >= 0) & (z < lines))
            def _():
                act(z, sign)

    from_line(own_index, True, line < lines - 1, line > 0)
    for c in local_in:
        c.start()

    def head_start():
        for step in range(1, peers):
            to = lax.rem(place + step, peers)
            for c in inner_copies(to, step, place, to):
                c.start()

    for distance in range(lines):
        if distance:

            def take(z, sign):
                index = block(row_y, z, col)
                for w in range(2):
                    arrived(w, index)
                up = (line < lines - 1) if sign < 0 else None
                down = (line > 0) if sign > 0 else None
                from_line(index, False, up, down)

            at_distance(distance, take)
        if distance == max(0, lines - 2):
            head_start()
        if distance == 0:
            from_plane(line)
            for c in local_in:
                c.wait()
            for c in local_out:
                c.start()
        else:
            at_distance(distance, lambda z, sign: from_plane(z))

    last_plane(line)
    for distance in range(1, lines):
        at_distance(distance, lambda z, sign: last_plane(z))

    for y in range(2):
        for z in range(lines):
            for x in range(cols):
                for w in range(2):
                    arrived(w, block(y, z, x, 1 - core))
    for step in range(1, peers):
        source = lax.rem(place + peers - step, peers)
        for c in inner_copies(place, step, source, source):
            c.wait_recv()
        for c in inner_copies(lax.rem(place + step, peers), step, place, source):
            c.wait_send()
    for c in local_out:
        c.wait()

    def sent_wait(which, index, way):
        copy(which, index, way, core_peer, False).wait_send()

    for z in range(lines):
        index = block(row_y, z, col)
        for w in range(2):
            for way in (XWAY, YWAY):
                sent_wait(w, index, way)

            @pl.when((z <= line) & (line < lines - 1))
            def _():
                sent_wait(w, index, UP)

            @pl.when((z >= line) & (line > 0))
            def _():
                sent_wait(w, index, DOWN)

        sent_wait(0, block(row_y, z, other_x), YWAY)
        sent_wait(1, block(other_y, z, col), XWAY)
        for y in range(2):
            for x in range(cols):
                for w in range(2):
                    sent_wait(w, block(y, z, x), CORE)


def spread(first, second, queries, attn_out, keys, values, devices, peers, cols):
    tokens = first.shape[0]
    head_width = queries.shape[1] // peers
    any_space = pl.BlockSpec(memory_space=pl.ANY)
    kind = first.dtype
    shapes = (
        jax.ShapeDtypeStruct((devices,) + first.shape, kind),
        jax.ShapeDtypeStruct((devices,) + second.shape, kind),
        jax.ShapeDtypeStruct((peers * tokens, head_width), kind),
        jax.ShapeDtypeStruct((peers * tokens, head_width), kind),
        jax.ShapeDtypeStruct((peers * tokens, HEAD_SIZE), kind),
        jax.ShapeDtypeStruct((peers * tokens, HEAD_SIZE), kind),
    )
    return pl.pallas_call(
        functools.partial(spread_kernel, cols, peers // cols),
        out_shape=shapes,
        in_specs=[any_space] * 6,
        out_specs=[any_space] * 6,
        scratch_shapes=[
            pltpu.VMEM(first.shape, kind),
            pltpu.VMEM(second.shape, kind),
            pltpu.VMEM((2, tokens, head_width), kind),
            pltpu.VMEM((2, tokens, HEAD_SIZE), kind),
            pltpu.SemaphoreType.DMA((2, 5, devices)),
            pltpu.SemaphoreType.DMA((2, devices)),
            pltpu.SemaphoreType.DMA((4,)),
            pltpu.SemaphoreType.DMA((4, peers)),
            pltpu.SemaphoreType.DMA((4, peers)),
            pltpu.SemaphoreType.DMA((8,)),
        ],
        compiler_params=pltpu.CompilerParams(
            collective_id=0, has_side_effects=True, vmem_limit_bytes=56 * 2**20
        ),
        cost_estimate=pl.CostEstimate(
            flops=0, bytes_accessed=500 * 2**20, transcendentals=0
        ),
    )(first, second, queries, attn_out, keys, values)


META_LANES = 128


def pick_kernel(expert_ref, first_ref, second_ref, inputs_ref, grads_ref):
    width = inputs_ref.shape[1]
    capacity = inputs_ref.shape[0]
    tokens, first_width = first_ref.shape
    topk = expert_ref[1]
    meta = first_ref[:, first_width - META_LANES :]
    lane = lax.broadcasted_iota(jnp.int32, (tokens, META_LANES), 1)
    chosen = jnp.where(
        (meta.astype(jnp.float32) == expert_ref[0].astype(jnp.float32)) & (lane < topk), 1.0, 0.0
    )
    source = lax.broadcasted_iota(jnp.int32, (META_LANES, META_LANES), 0)
    target = lax.broadcasted_iota(jnp.int32, (META_LANES, META_LANES), 1)
    away = source - target
    fold = (
        (target < topk) & ((away == topk) | (away == 2 * topk) | (away == 3 * topk))
    ).astype(jnp.float32).astype(jnp.bfloat16)
    gates = jnp.dot(meta, fold, preferred_element_type=jnp.float32)
    weight = jnp.sum(chosen * gates, axis=1, keepdims=True)
    named = contract_last(jnp.ones((8, META_LANES), jnp.bfloat16), chosen.astype(jnp.bfloat16))
    row = lax.broadcasted_iota(jnp.int32, (tokens, tokens), 0)
    column = lax.broadcasted_iota(jnp.int32, (tokens, tokens), 1)
    before = (row < column).astype(jnp.float32).astype(jnp.bfloat16)
    rank = jnp.dot(named.astype(jnp.bfloat16), before, preferred_element_type=jnp.float32)
    slot = lax.broadcasted_iota(jnp.int32, (capacity, tokens), 0).astype(jnp.float32)
    pick = jnp.where((slot == rank[:1]) & (named[:1] > 0.5), 1.0, 0.0).astype(jnp.bfloat16)

    def picked(rows):
        return jnp.dot(pick, rows, preferred_element_type=jnp.float32).astype(jnp.bfloat16)

    def scaled(rows):
        return (rows.astype(jnp.float32) * weight).astype(jnp.bfloat16)

    extra = first_width - META_LANES - width
    inputs_ref[...] = picked(first_ref[:, :width])
    grads_ref[:, :extra] = picked(scaled(first_ref[:, width : width + extra]))
    grads_ref[:, extra:] = picked(scaled(second_ref[...]))


def pick_rows(expert, topk, first_all, second_all, capacity, width):
    devices, tokens, first_width = first_all.shape
    second_width = second_all.shape[2]
    out = jax.ShapeDtypeStruct((devices * capacity, width), first_all.dtype)
    return pl.pallas_call(
        pick_kernel,
        grid_spec=pltpu.PrefetchScalarGridSpec(
            num_scalar_prefetch=1,
            grid=(devices,),
            in_specs=[
                pl.BlockSpec((None, tokens, first_width), lambda d, e: (d, 0, 0)),
                pl.BlockSpec((None, tokens, second_width), lambda d, e: (d, 0, 0)),
            ],
            out_specs=[pl.BlockSpec((capacity, width), lambda d, e: (d, 0))] * 2,
        ),
        out_shape=(out, out),
        compiler_params=pltpu.CompilerParams(vmem_limit_bytes=56 * 2**20),
    )(jnp.stack([expert, jnp.int32(topk)]), first_all, second_all)


def slot_ranks(named):
    tokens = named.shape[1]
    before = jnp.triu(jnp.ones((tokens, tokens), jnp.bfloat16), 1)
    return jnp.dot(named.astype(jnp.bfloat16), before, preferred_element_type=jnp.float32).astype(
        jnp.int32
    )


def per_device(
    grad_out,
    hidden,
    norm_gain,
    expert_ids,
    gate_weights,
    w_gate,
    w_up,
    w_down,
    w_out,
    queries,
    keys,
    values,
    attn_out,
    lse,
):
    token_rows, width = hidden.shape
    topk = expert_ids.shape[1]
    groups = lax.axis_size("grp")
    inner_product = lax.axis_size("inner")
    experts_all = w_gate.shape[0] * groups * inner_product
    capacity = max(2, 5 * token_rows * topk // (4 * experts_all))
    hidden_f = hidden.astype(jnp.float32)
    inverse = lax.rsqrt(jnp.mean(hidden_f * hidden_f, axis=1, keepdims=True) + EPSILON)
    normed = (hidden_f * inverse * norm_gain).astype(jnp.bfloat16)
    upstream = grad_out.astype(jnp.float32)
    cols = groups // 2
    devices = groups * inner_product
    gather_plan = (
        cols == 2
        and inner_product % cols == 0
        and w_gate.shape[0] == 1
        and experts_all <= 256
        and 4 * topk <= META_LANES
        and 2 * devices * hidden.size * hidden.dtype.itemsize <= GATHER_LIMIT
    )
    if gather_plan:
        high = lax.reduce_precision(gate_weights, 8, 7)
        middle = lax.reduce_precision(gate_weights - high, 8, 7)
        low = gate_weights - high - middle
        extra = width // 4
        blank = jnp.zeros((token_rows, META_LANES - 4 * topk), jnp.bfloat16)
        first = jnp.concatenate(
            [
                normed,
                grad_out[:, :extra],
                expert_ids.astype(jnp.bfloat16),
                high.astype(jnp.bfloat16),
                middle.astype(jnp.bfloat16),
                low.astype(jnp.bfloat16),
                blank,
            ],
            axis=1,
        )
        first_all, second_all, head_query, head_output, head_key, head_value = spread(
            first,
            grad_out[:, extra:],
            queries,
            attn_out,
            keys,
            values,
            devices,
            inner_product,
            cols,
        )
        expert = lax.axis_index("grp") * inner_product + lax.axis_index("inner")
        slot_inputs, slot_grads = pick_rows(
            expert, topk, first_all, second_all, capacity, width
        )
        row_parts = expert_rows_grads(
            slot_inputs, slot_grads, w_gate[0], w_up[0], w_down[0]
        )
        returned = [
            lax.all_to_all(part, ("grp", "inner"), split_axis=0, concat_axis=0, tiled=True)
            for part in row_parts
        ]
        mine = jnp.any(
            expert_ids.T[None] == jnp.arange(experts_all, dtype=jnp.int32)[:, None, None], axis=1
        )
        place = (
            (
                jnp.arange(capacity, dtype=jnp.int32)[None, :, None]
                == slot_ranks(mine)[:, None, :]
            )
            & mine[:, None, :]
        ).astype(jnp.bfloat16)
        place = place.reshape(experts_all * capacity, token_rows)
        grad_normed = jnp.concatenate(
            [contract_first(place, part) for part in returned], axis=1
        )
    else:
        flat_count = token_rows * topk
        flat_ids = expert_ids.reshape(-1)
        one_hot = (flat_ids[:, None] == jnp.arange(experts_all, dtype=jnp.int32)[None, :]).astype(
            jnp.int32
        )
        slot_rank = jnp.sum((jnp.cumsum(one_hot, axis=0) - one_hot) * one_hot, axis=1)
        target = flat_ids * capacity + slot_rank
        owner = (
            jnp.full((experts_all * capacity,), flat_count, jnp.int32)
            .at[target]
            .set(jnp.arange(flat_count, dtype=jnp.int32))
        )
        source_tok = owner // topk
        scaled = (
            (upstream[:, None, :] * gate_weights[:, :, None])
            .reshape(flat_count, width)
            .astype(jnp.bfloat16)
        )
        zero_row = jnp.zeros((1, width), jnp.bfloat16)
        slot_inputs = jnp.concatenate([normed, zero_row], axis=0)[source_tok]
        slot_grads = jnp.concatenate([scaled, zero_row], axis=0)[owner]
        outgoing = jnp.concatenate([slot_inputs, slot_grads], axis=1).reshape(
            experts_all, capacity, 2 * width
        )
        returned = lax.all_to_all(
            expert_grads(
                lax.all_to_all(outgoing, ("grp", "inner"), split_axis=0, concat_axis=0, tiled=True),
                w_gate,
                w_up,
                w_down,
            ),
            ("grp", "inner"),
            split_axis=0,
            concat_axis=0,
            tiled=True,
        )
        expert_rows = returned.reshape(-1, width)[target].astype(jnp.float32)
        grad_normed = jnp.sum(expert_rows.reshape(token_rows, topk, width), axis=1)
    gained = grad_normed * norm_gain
    statistic = jnp.mean(gained * hidden_f, axis=1, keepdims=True)
    grad_resid = (
        upstream + inverse * gained - hidden_f * inverse * inverse * inverse * statistic
    ).astype(jnp.bfloat16)
    head_width = queries.shape[1] // inner_product
    per_head = head_width // HEAD_SIZE
    shared_portion = inner_product // KEY_VALUE_HEADS
    if not gather_plan:
        key_value_pairs = jnp.concatenate(
            [
                keys.reshape(token_rows, KEY_VALUE_HEADS, 1, HEAD_SIZE),
                values.reshape(token_rows, KEY_VALUE_HEADS, 1, HEAD_SIZE),
            ],
            axis=2,
        )
        key_value_broadcast = jnp.broadcast_to(
            key_value_pairs[:, :, None], (token_rows, KEY_VALUE_HEADS, shared_portion, 2, HEAD_SIZE)
        ).reshape(token_rows, inner_product * 2 * HEAD_SIZE)
        head_query, head_output, head_kv = (
            lax.all_to_all(queries, "inner", split_axis=1, concat_axis=0, tiled=True),
            lax.all_to_all(attn_out, "inner", split_axis=1, concat_axis=0, tiled=True),
            lax.all_to_all(key_value_broadcast, "inner", split_axis=1, concat_axis=0, tiled=True),
        )
    head_grad = contract_last(
        lax.all_gather(grad_resid, "inner", axis=0, tiled=True), w_out
    ).astype(jnp.bfloat16)
    seq_len = head_query.shape[0]
    if not gather_plan:
        head_key = head_kv[:, :HEAD_SIZE]
        head_value = head_kv[:, HEAD_SIZE:]
    lse_rows = lse.T
    scale = float(HEAD_SIZE) ** (-0.5)
    blocks = 1
    while blocks < 8 and seq_len % (2 * blocks) == 0 and (seq_len // (2 * blocks) >= 512):
        blocks = blocks * 2
    block_len = seq_len // blocks
    grad_key_acc = jnp.zeros((seq_len, HEAD_SIZE), jnp.float32)
    grad_value_acc = jnp.zeros((seq_len, HEAD_SIZE), jnp.float32)
    query_parts = []
    for block_index in range(blocks):
        low = block_index * block_len
        high = low + block_len
        block_query = head_query[low:high].reshape(block_len * per_head, HEAD_SIZE)
        block_output = head_output[low:high].reshape(block_len * per_head, HEAD_SIZE)
        block_grad = head_grad[low:high].reshape(block_len * per_head, HEAD_SIZE)
        block_lse = lse_rows[low:high].reshape(-1)
        seen_key = head_key[:high]
        seen_value = head_value[:high]
        scores = contract_last(block_query, seen_key) * scale
        row_position = low + jnp.arange(block_len * per_head, dtype=jnp.int32) // per_head
        visible = jnp.arange(high, dtype=jnp.int32)[None, :] <= row_position[:, None]
        probs = jnp.where(visible, jnp.exp(scores - block_lse[:, None]), 0.0)
        grad_probs = contract_last(block_grad, seen_value)
        delta = jnp.sum(
            block_grad.astype(jnp.float32) * block_output.astype(jnp.float32), axis=1, keepdims=True
        )
        grad_scores = (probs * (grad_probs - delta)).astype(jnp.bfloat16)
        query_part = jnp.dot(grad_scores, seen_key, preferred_element_type=jnp.float32) * scale
        query_parts.append(query_part.reshape(block_len, head_width))
        grad_key_acc = grad_key_acc.at[:high].add(contract_first(grad_scores, block_query) * scale)
        grad_value_acc = grad_value_acc.at[:high].add(
            contract_first(probs.astype(jnp.bfloat16), block_grad)
        )
    grad_query_heads = jnp.concatenate(query_parts, axis=0)
    kv_heads = jnp.concatenate([grad_key_acc, grad_value_acc], axis=1)
    token_query, token_key_value = (
        lax.all_to_all(
            grad_query_heads.astype(jnp.bfloat16), "inner", split_axis=0, concat_axis=1, tiled=True
        ).astype(grad_query_heads.dtype),
        lax.all_to_all(
            kv_heads.astype(jnp.bfloat16), "inner", split_axis=0, concat_axis=1, tiled=True
        ).astype(kv_heads.dtype),
    )
    summed_total = jnp.sum(
        token_key_value.reshape(token_rows, KEY_VALUE_HEADS, shared_portion, 2, HEAD_SIZE), axis=2
    )
    keys_gradient = (
        summed_total[:, :, 0].reshape(token_rows, KEY_VALUE_HEADS * HEAD_SIZE).astype(jnp.bfloat16)
    )
    values_gradient = (
        summed_total[:, :, 1].reshape(token_rows, KEY_VALUE_HEADS * HEAD_SIZE).astype(jnp.bfloat16)
    )
    return (grad_resid, token_query.astype(jnp.bfloat16), keys_gradient, values_gradient)


def solution(mesh):
    placed = (
        P(("grp", "inner"), None),
        P(("grp", "inner"), None),
        P(),
        P(("grp", "inner"), None),
        P(("grp", "inner"), None),
        P(("grp", "inner"), None, None),
        P(("grp", "inner"), None, None),
        P(("grp", "inner"), None, None),
        P("inner", None),
        P(("grp", "inner"), None),
        P(("grp", "inner"), None),
        P(("grp", "inner"), None),
        P(("grp", "inner"), None),
        P("inner", "grp"),
    )
    return jax.shard_map(
        per_device,
        mesh=mesh,
        in_specs=placed,
        out_specs=(
            P(("grp", "inner"), None),
            P(("grp", "inner"), None),
            P(("grp", "inner"), None),
            P(("grp", "inner"), None),
        ),
        check_vma=False,
    )
```
